256 devices in a mesh: gx: 32 (over y, z), gy: 8 (over x, core).
Axes of the slice: x: 4, y: 4, z: 8, core: 2. Of those that a mesh axis runs over, the one named last changes fastest.
Arguments:
- operators: float32 [32, 8, 1536, 1536], P('gx', 'gy'), may hold values from -0.15625 to 0.15625
- sources: float32 [32, 8, 5, 64, 128], P('gx', 'gy'), may hold values from -6 to 6
- source_rows: int32 [32, 8, 128], P('gx', 'gy'), may hold values from 0 to 1535
- batch_plan: int32 [5], replicated, may hold values from 0 to 4, each once
Outputs:
- traces: float32 [32, 8, 4, 64, 1536], P('gx', 'gy')
- basis: float32 [32, 8, 64, 1536], P('gx', 'gy')
- factor: float32 [64, 64], replicated
The draws below stay inside these ranges and needn't reach their ends.
Inputs may be any that keep to these rules, and one draw needn't show every extreme that they name: `batch_plan`: a permutation of the 5 source blocks.
All inputs are finite; a program needn't handle non-finite values.
Results may differ from the reference program's by a relative error of at most 0.0003.
Values sent between devices are 32-bit elements; how exact they have to be, the bound alone decides.
No kernel may reach another device: no remote copies, remote signals or barrier semaphores. Data moves between devices by JAX's collectives and lax.ppermute only.
A program may use at most 64 MiB of HBM per device.

```python
import jax
import jax.numpy as jnp
from jax import lax

ORDER = 1536
COLS = 64
NB = 5
NSRC = 128
SUBX = 32
SUBY = 8
ROWS = 393216


def with_ends(drawn, own_key, smallest, top_value):
    dims = drawn.shape
    place = [jax.random.randint(jax.random.fold_in(own_key, axis), (), 0, dims[axis]) for axis in range(len(dims))]
    drawn = drawn.at[tuple(place)].set(smallest)
    longest = dims.index(max(dims))
    place[longest] = (place[longest] + 1) % dims[longest]
    return drawn.at[tuple(place)].set(top_value)


def shard_levels(stream_key, dims, split, least, top_value):
    loudness, own = 1.0, jax.random.fold_in(stream_key, 6)
    for axis_at, blocks in split:
        heights = jnp.exp(jax.random.uniform(jax.random.fold_in(own, axis_at), (blocks,), jnp.float32, least / len(split), top_value / len(split)))
        loudness = loudness * jnp.repeat(heights, dims[axis_at] // blocks).reshape([-1 if axis == axis_at else 1 for axis in range(len(dims))])
    return loudness


def gaussian(key, dims, width, most, split=(), kind=jnp.bfloat16):
    loudness = shard_levels(key, dims, split, -0.22, 0.18) if split else 1.0
    entries = jax.random.normal(key, dims, jnp.float32) * width * loudness
    return jnp.minimum(jnp.maximum(entries, -most), most).astype(kind)


def setup_inputs(seed: int = 0) -> dict:
    arg_keys = jax.random.split(jax.random.key(seed), 5)
    return {
        "operators": gaussian(arg_keys[0], (SUBX, SUBY, ORDER, ORDER), ORDER ** -0.5, 0.15625, ((0, 32), (1, 8)), jnp.float32),
        "sources": gaussian(arg_keys[1], (SUBX, SUBY, NB, COLS, NSRC), 1.0, 6.0, ((0, 32), (1, 8)), jnp.float32),
        "source_rows": with_ends(jax.random.randint(arg_keys[2], (SUBX, SUBY, NSRC), 0, ORDER), jax.random.fold_in(arg_keys[2], 1), 0, ORDER - 1).astype(jnp.int32),
        "batch_plan": jax.random.permutation(arg_keys[3], NB).astype(jnp.int32),
    }


def reference(operators, sources, source_rows, batch_plan):
    ordered = jnp.take(sources, batch_plan, axis=2)
    total_rows = NB * COLS
    half = ORDER // 2

    def column(west_all, col_index):

        def cell(south_in, row_index):
            trace_map = operators[col_index, row_index]
            source = ordered[col_index, row_index].reshape(total_rows, NSRC)
            placing = (source_rows[col_index, row_index][:, None] == jnp.arange(ORDER, dtype=jnp.int32)[None, :]).astype(jnp.float32)
            joined = jnp.concatenate([west_all[row_index], south_in], axis=1)
            outgoing = jnp.dot(joined.astype(jnp.float32), trace_map.astype(jnp.float32), precision=lax.Precision.HIGHEST, preferred_element_type=jnp.float32)
            outgoing = outgoing + jnp.dot(source.astype(jnp.float32), placing.astype(jnp.float32), precision=lax.Precision.HIGHEST, preferred_element_type=jnp.float32)
            return (outgoing[:, half:], outgoing)
        start = jnp.zeros((total_rows, half), jnp.float32)
        _, outs = lax.scan(cell, start, jnp.arange(SUBY, dtype=jnp.int32))
        return (outs[:, :, :half], outs)
    west_start = jnp.zeros((SUBY, total_rows, half), jnp.float32)
    _, grid = lax.scan(column, west_start, jnp.arange(SUBX, dtype=jnp.int32))
    grid = grid.reshape(SUBX, SUBY, NB, COLS, ORDER)
    first = grid[:, :, 0]
    traces = grid[:, :, 1:]
    gram = jnp.einsum('xyco,xydo->cd', first, first, precision=lax.Precision.HIGHEST) / ROWS
    lower = jnp.linalg.cholesky(gram)
    flat = jnp.transpose(first, (2, 0, 1, 3)).reshape(COLS, SUBX * SUBY * ORDER)
    solved = jax.scipy.linalg.solve_triangular(lower, flat, lower=True)
    basis = jnp.transpose(solved.reshape(COLS, SUBX, SUBY, ORDER), (1, 2, 0, 3))
    return (traces, basis, lower.T)
```

```python
import functools

import jax
import jax.numpy as jnp
from jax import lax
from jax.experimental import pallas as pl
from jax.experimental.pallas import tpu as pltpu
from jax.sharding import PartitionSpec as P

PIECES = 2
UNROLL = 8
VMEM = pl.BlockSpec(memory_space=pltpu.VMEM)
SMEM = pl.BlockSpec(memory_space=pltpu.SMEM)
HBM = pl.BlockSpec(memory_space=pltpu.HBM)
F32 = jnp.float32
BF16 = jnp.bfloat16


def halves(value):
    high = value.astype(BF16)
    low = (value - high.astype(F32)).astype(BF16)
    return high, low


def product(value, high_ref, low_ref):
    rows = value.shape[0]
    high, low = halves(value)
    both = jnp.concatenate([high, low], axis=0)
    main = jnp.dot(both, high_ref[...], preferred_element_type=F32)
    rest = jnp.dot(high, low_ref[...], preferred_element_type=F32)
    return main[:rows] + (main[rows:] + rest)


def held(value):
    return pltpu.with_memory_space_constraint(value, pltpu.VMEM)


def params(mib):
    return pltpu.CompilerParams(vmem_limit_bytes=mib << 20)


def split_kernel(chunk, w_hbm, high_ref, low_ref, buf, sem):
    count = w_hbm.shape[0] // chunk

    def fetch(i):
        return pltpu.make_async_copy(
            w_hbm.at[pl.ds(i * chunk, chunk)], buf.at[i % 2], sem.at[i % 2]
        )

    fetch(0).start()
    for i in range(count):
        if i + 1 < count:
            fetch(i + 1).start()
        fetch(i).wait()
        high, low = halves(buf[i % 2])
        high_ref[i * chunk : (i + 1) * chunk, :] = high
        low_ref[i * chunk : (i + 1) * chunk, :] = low


def split_operator(w):
    order = w.shape[0]
    chunk = order // 6
    shape = pltpu.VMEM((order, order), BF16)
    return pl.pallas_call(
        functools.partial(split_kernel, chunk),
        out_shape=(shape, shape),
        in_specs=[HBM],
        out_specs=(VMEM, VMEM),
        scratch_shapes=[
            pltpu.VMEM((2, chunk, order), F32),
            pltpu.SemaphoreType.DMA((2,)),
        ],
        compiler_params=params(16),
        name="split_operator",
    )(w)


def when_active(offset, count, age_ref):
    age = age_ref[0] + offset
    piece = lax.div(age, 2)
    return (age >= 0) & (age < 2 * count) & (age == 2 * piece), piece


def south_kernel(offset, count, age_ref, placed_ref, south_ref, high_ref, low_ref, out_ref):
    active, piece = when_active(offset, count, age_ref)
    half = south_ref.shape[1]

    @pl.when(active)
    def _():
        out_ref[...] = placed_ref[piece] + product(
            south_ref[...], high_ref.at[half:, :], low_ref.at[half:, :]
        )


def west_kernel(offset, count, first, age_ref, partial_ref, west_ref, high_ref, low_ref, *refs):
    out_ref = refs[-1]
    active, _ = when_active(offset, count, age_ref)
    half = west_ref.shape[1]
    cols = slice(first, first + half)

    @pl.when(active)
    def _():
        out_ref[...] = partial_ref[:, cols] + product(
            west_ref[...], high_ref.at[:half, cols], low_ref.at[:half, cols]
        )


def south_part(offset, count, age, placed, south, high, low):
    _, width, order = placed.shape
    return pl.pallas_call(
        functools.partial(south_kernel, offset, count),
        out_shape=jax.ShapeDtypeStruct((width, order), F32),
        in_specs=[SMEM] + [VMEM] * 4,
        out_specs=VMEM,
        compiler_params=params(4),
        cost_estimate=pl.CostEstimate(flops=6 * width * order * order // 2, bytes_accessed=1 << 20, transcendentals=0),
        name="south",
    )(age, held(placed), south, held(high), held(low))


def west_part(offset, count, first, age, partial, west, high, low, after=()):
    width, half = west.shape
    return pl.pallas_call(
        functools.partial(west_kernel, offset, count, first),
        out_shape=jax.ShapeDtypeStruct((width, half), F32),
        in_specs=[SMEM] + [VMEM] * (4 + len(after)),
        out_specs=VMEM,
        compiler_params=params(4),
        cost_estimate=pl.CostEstimate(flops=6 * width * half * half, bytes_accessed=1 << 20, transcendentals=0),
        name="north" if first else "east",
    )(age, partial, west, held(high), held(low), *after)


def place_kernel(plan_ref, rows_ref, sources_ref, out_ref):
    batches, columns, placed_count = sources_ref.shape
    order = out_ref.shape[-1]
    at = lax.broadcasted_iota(jnp.int32, (order, placed_count), 0)
    placing = jnp.where(at == rows_ref[...], 1.0, 0.0).astype(BF16)
    for b in range(batches):
        source = sources_ref[plan_ref[b]]
        high, middle = halves(source)
        low = (source - high.astype(F32) - middle.astype(F32)).astype(BF16)
        parts = jnp.concatenate([high, middle, low], axis=0)
        spread = lax.dot_general(
            parts, placing, (((1,), (1,)), ((), ())), preferred_element_type=F32
        )
        out_ref[b] = spread[:columns] + (
            spread[columns : 2 * columns] + spread[2 * columns :]
        )


def place(plan, rows, sources, order):
    batches, columns, _ = sources.shape
    return pl.pallas_call(
        place_kernel,
        out_shape=pltpu.VMEM((batches, columns, order), F32),
        in_specs=[SMEM, VMEM, VMEM],
        out_specs=VMEM,
        compiler_params=params(8),
        name="place",
    )(plan, rows, sources)


def sweep_pairs(shape, parity, dx, dy):
    nx, ny = shape
    return [
        (x * ny + y, (x + dx) * ny + y + dy)
        for x in range(parity, nx - dx, 2)
        for y in range(ny - dy)
    ]


def body(shape, operators, sources, source_rows, batch_plan):
    nx, ny = shape
    axes = ("gx", "gy")
    depth = lax.axis_index("gx") + 2 * lax.axis_index("gy")
    order = operators.shape[-1]
    half = order // 2
    _, _, batches, columns, placed_count = sources.shape
    width = columns // PIECES
    count = batches * PIECES
    placed = place(batch_plan, source_rows[0], sources[0, 0], order)
    placed = placed.reshape(count, width, order)
    high, low = split_operator(operators[0, 0])

    halves_needed = nx - 1 + 2 * (ny - 1) + 2 * (count - 1) + 1
    trips = -(-halves_needed // (2 * UNROLL))

    def advance(trip, carry):
        west, south, results = carry
        west, south = list(west), list(south)
        age = trip * (2 * UNROLL) - depth
        age_ref = age[None].astype(jnp.int32)
        for offset in range(2 * UNROLL):
            parity = offset % 2
            partial = south_part(offset, count, age_ref, placed, south[parity], high, low)
            to_east = west_part(offset, count, 0, age_ref, partial, west[parity], high, low)
            west[1 - parity] = lax.ppermute(
                to_east, axes, sweep_pairs(shape, parity, 1, 0)
            )
            to_north = west_part(
                offset, count, half, age_ref, partial, west[parity], high, low, (to_east,)
            )
            south[parity] = lax.ppermute(
                to_north, axes, sweep_pairs(shape, parity, 0, 1)
            )
            now = age + offset
            active = (now >= 0) & (now < 2 * count) & (now % 2 == 0)
            slot = jnp.where(active, now // 2 + 1, 0)
            results = lax.dynamic_update_slice(results, to_east[None], (slot, 0, 0))
            results = lax.dynamic_update_slice(results, to_north[None], (slot, 0, half))
        return (tuple(west), tuple(south), results)

    zero = jnp.zeros((width, half), F32)
    carry = ((zero, zero), (zero, zero), jnp.zeros((count + 1, width, order), F32))
    _, _, results = lax.fori_loop(0, trips, advance, carry)
    first = results[1 : 1 + PIECES].reshape(columns, order)
    rest = results[1 + PIECES :]
    partial_gram = lax.dot_general(
        first,
        first,
        (((1,), (1,)), ((), ())),
        precision=lax.Precision.HIGHEST,
        preferred_element_type=F32,
    )
    gram = lax.psum(partial_gram, axes) / (nx * ny * order)
    lower = jnp.linalg.cholesky(gram)
    basis = jax.scipy.linalg.solve_triangular(lower, first, lower=True)
    traces = rest.reshape(batches - 1, columns, order)
    return (traces[None, None], basis[None, None], lower.T)


def solution(mesh):
    return jax.shard_map(
        functools.partial(body, (mesh.shape["gx"], mesh.shape["gy"])),
        mesh=mesh,
        in_specs=(
            P("gx", "gy", None, None),
            P("gx", "gy", None, None, None),
            P("gx", "gy", None),
            P(),
        ),
        out_specs=(P("gx", "gy", None, None, None), P("gx", "gy", None, None), P()),
        check_vma=False,
    )
```

```python
import functools

import jax
import jax.numpy as jnp
from jax import lax
from jax.experimental import pallas as pl
from jax.experimental.pallas import tpu as pltpu
from jax.sharding import PartitionSpec as P

PIECES = 2
UNROLL = 7
Z = 8
LIMIT = 8
VMEM = pl.BlockSpec(memory_space=pltpu.VMEM)
SMEM = pl.BlockSpec(memory_space=pltpu.SMEM)
HBM = pl.BlockSpec(memory_space=pltpu.HBM)
ANY = pl.BlockSpec(memory_space=pl.ANY)
F32 = jnp.float32
BF16 = jnp.bfloat16


def halves(value):
    high = value.astype(BF16)
    low = (value - high.astype(F32)).astype(BF16)
    return high, low


def product(value, high_ref, low_ref):
    rows = value.shape[0]
    high, low = halves(value)
    both = jnp.concatenate([high, low], axis=0)
    main = jnp.dot(both, high_ref[...], preferred_element_type=F32)
    rest = jnp.dot(high, low_ref[...], preferred_element_type=F32)
    return main[:rows] + (main[rows:] + rest)


def pass_through_kernel(*refs):
    del refs


def pass_through(*arrays):
    return pl.pallas_call(
        pass_through_kernel,
        out_shape=tuple(jax.ShapeDtypeStruct(a.shape, a.dtype) for a in arrays),
        in_specs=[ANY] * len(arrays),
        out_specs=(ANY,) * len(arrays),
        input_output_aliases={i: i for i in range(len(arrays))},
        compiler_params=params(4),
        name="pass_through",
    )(*arrays)


def params(mib):
    return pltpu.CompilerParams(vmem_limit_bytes=mib << 20)


def split_kernel(chunk, w_hbm, *refs):
    quarters, (buf, sem) = refs[:8], refs[8:]
    half = w_hbm.shape[0] // 2
    count = 2 * half // chunk

    def fetch(i):
        return pltpu.make_async_copy(
            w_hbm.at[pl.ds(i * chunk, chunk)], buf.at[i % 2], sem.at[i % 2]
        )

    fetch(0).start()
    for i in range(count):
        if i + 1 < count:
            fetch(i + 1).start()
        fetch(i).wait()
        high, low = halves(buf[i % 2])
        side, at = divmod(i * chunk, half)
        for j in range(2):
            cols = slice(j * half, (j + 1) * half)
            quarters[4 * side + 2 * j][at : at + chunk, :] = high[:, cols]
            quarters[4 * side + 2 * j + 1][at : at + chunk, :] = low[:, cols]


def split_operator(w):
    order = w.shape[0]
    half = order // 2
    chunk = half // 3
    shape = jax.ShapeDtypeStruct((half, half), BF16)
    return pl.pallas_call(
        functools.partial(split_kernel, chunk),
        out_shape=(shape,) * 8,
        in_specs=[HBM],
        out_specs=(VMEM,) * 8,
        scratch_shapes=[
            pltpu.VMEM((2, chunk, order), F32),
            pltpu.SemaphoreType.DMA((2,)),
        ],
        compiler_params=params(16),
        name="split_operator",
    )(w)


def when_active(offset, count, age_ref):
    age = age_ref[0] + offset
    piece = lax.div(age, 2)
    return (age >= 0) & (age < 2 * count) & (age == 2 * piece), piece


def south_kernel(offset, count, age_ref, placed_ref, south_ref, eh_ref, el_ref, nh_ref, nl_ref, out_ref):
    active, piece = when_active(offset, count, age_ref)
    half = south_ref.shape[1]

    @pl.when(active)
    def _():
        south = south_ref[...]
        out_ref[:, :half] = placed_ref[piece, :, :half] + product(south, eh_ref, el_ref)
        out_ref[:, half:] = placed_ref[piece, :, half:] + product(south, nh_ref, nl_ref)


def chosen(age_ref, west_refs):
    if len(west_refs) == 1:
        return west_refs[0][...]
    return jnp.where(age_ref[1] > 0, west_refs[1][...], west_refs[0][...])


def east_kernel(offset, count, wests, age_ref, partial_ref, high_ref, low_ref, *refs):
    active, _ = when_active(offset, count, age_ref)
    west_refs, (out_ref,) = refs[:wests], refs[wests:]
    half = out_ref.shape[1]

    @pl.when(active)
    def _():
        west = chosen(age_ref, west_refs)
        out_ref[...] = partial_ref[:, :half] + product(west, high_ref, low_ref)


def north_kernel(offset, count, wests, age_ref, partial_ref, high_ref, low_ref, *refs):
    west_refs, (east_ref, _, out_ref, results_ref) = refs[:wests], refs[wests:]
    active, piece = when_active(offset, count, age_ref)
    half = out_ref.shape[1]

    @pl.when(active)
    def _():
        west = chosen(age_ref, west_refs)
        value = partial_ref[:, half:] + product(west, high_ref, low_ref)
        out_ref[...] = value
        results_ref[piece, :, :half] = east_ref[...]
        results_ref[piece, :, half:] = value


def estimate(width, half, quarters):
    return pl.CostEstimate(
        flops=6 * quarters * width * half * half,
        bytes_accessed=1 << 20,
        transcendentals=0,
    )


def south_part(offset, count, age, placed, south, weights):
    _, width, order = placed.shape
    return pl.pallas_call(
        functools.partial(south_kernel, offset, count),
        out_shape=jax.ShapeDtypeStruct((width, order), F32),
        in_specs=[SMEM] + [VMEM] * 6,
        out_specs=VMEM,
        compiler_params=params(LIMIT),
        cost_estimate=estimate(width, order // 2, 2),
        name="south",
    )(age, placed, south, *weights)


def east_part(offset, count, age, partial, wests, weights):
    width, half = wests[0].shape
    return pl.pallas_call(
        functools.partial(east_kernel, offset, count, len(wests)),
        out_shape=jax.ShapeDtypeStruct((width, half), F32),
        in_specs=[SMEM] + [VMEM] * (3 + len(wests)),
        out_specs=VMEM,
        compiler_params=params(LIMIT),
        cost_estimate=estimate(width, half, 1),
        name="east",
    )(age, partial, *weights, *wests)


def north_part(offset, count, age, partial, wests, weights, east, results):
    width, half = wests[0].shape
    return pl.pallas_call(
        functools.partial(north_kernel, offset, count, len(wests)),
        out_shape=(
            jax.ShapeDtypeStruct((width, half), F32),
            jax.ShapeDtypeStruct(results.shape, F32),
        ),
        in_specs=[SMEM] + [VMEM] * (5 + len(wests)),
        out_specs=(VMEM, VMEM),
        input_output_aliases={5 + len(wests): 1},
        compiler_params=params(LIMIT),
        cost_estimate=estimate(width, half, 1),
        name="north",
    )(age, partial, *weights, *wests, east, results)


def summed(value, shape):
    for axis, size in (("gy", shape[1]), ("gx", shape[0])):
        apart = 1
        while apart < size:
            pairs = [(i, i ^ apart) for i in range(size)]
            value = value + lax.ppermute(value, axis, pairs)
            apart *= 2
    return value


def place_kernel(plan_ref, rows_ref, sources_ref, out_ref):
    batches, columns, placed_count = sources_ref.shape
    order = out_ref.shape[-1]
    at = lax.broadcasted_iota(jnp.int32, (order, placed_count), 0)
    placing = jnp.where(at == rows_ref[...], 1.0, 0.0).astype(BF16)
    for b in range(batches):
        source = sources_ref[plan_ref[b]]
        high, middle = halves(source)
        low = (source - high.astype(F32) - middle.astype(F32)).astype(BF16)
        parts = jnp.concatenate([high, middle, low], axis=0)
        spread = lax.dot_general(
            parts, placing, (((1,), (1,)), ((), ())), preferred_element_type=F32
        )
        out_ref[b] = spread[:columns] + (
            spread[columns : 2 * columns] + spread[2 * columns :]
        )


def place(plan, rows, sources, order):
    batches, columns, _ = sources.shape
    return pl.pallas_call(
        place_kernel,
        out_shape=jax.ShapeDtypeStruct((batches, columns, order), F32),
        in_specs=[SMEM, VMEM, VMEM],
        out_specs=VMEM,
        compiler_params=params(8),
        name="place",
    )(plan, rows, sources)


def east_pairs(shape, parity, far):
    nx, ny = shape
    return [
        (x * ny + y, (x + 1) * ny + y)
        for x in range(parity, nx - 1, 2)
        for y in range(ny)
        if ((x + 1) % Z == 0) == far
    ]


def north_pairs(shape, parity):
    nx, ny = shape
    return [
        (x * ny + y, x * ny + y + 1) for x in range(parity, nx, 2) for y in range(ny - 1)
    ]


def body(shape, operators, sources, source_rows, batch_plan):
    nx, ny = shape
    axes = ("gx", "gy")
    column = lax.axis_index("gx")
    depth = column + 2 * lax.div(column, Z) + 2 * lax.axis_index("gy")
    starts_row = (lax.rem(column, Z) == 0).astype(jnp.int32)
    order = operators.shape[-1]
    half = order // 2
    _, _, batches, columns, placed_count = sources.shape
    width = columns // PIECES
    count = batches * PIECES
    placed = place(batch_plan, source_rows[0], sources[0, 0], order)
    placed = placed.reshape(count, width, order)
    quarters = split_operator(operators[0, 0])

    deepest = nx - 1 + 2 * ((nx - 1) // Z) + 2 * (ny - 1)
    steps = (deepest + 2 * (count - 1)) // 2 + 1
    trips = -(-steps // UNROLL)

    def advance(trip, carry):
        even_west, odd_west, far_old, far_new, south, results, fixed = carry
        south = list(south)
        fixed = pass_through(*fixed)
        placed, quarters = fixed[0], fixed[1:]
        age = trip * (2 * UNROLL) - depth
        age_ref = jnp.stack([age, starts_row]).astype(jnp.int32)
        for offset in range(2 * UNROLL):
            parity = offset % 2
            wests = (odd_west,) if parity else (even_west, far_old)
            partial = south_part(
                offset, count, age_ref, placed, south[parity], quarters[4:]
            )
            to_east = east_part(offset, count, age_ref, partial, wests, quarters[:2])
            arrived = lax.ppermute(to_east, axes, east_pairs(shape, parity, False))
            to_north, results = north_part(
                offset, count, age_ref, partial, wests, quarters[2:4], to_east, results
            )
            south[parity] = lax.ppermute(to_north, axes, north_pairs(shape, parity))
            if parity:
                even_west = arrived
                far_old, far_new = far_new, lax.ppermute(
                    to_east, axes, east_pairs(shape, parity, True)
                )
            else:
                odd_west = arrived
        return (even_west, odd_west, far_old, far_new, tuple(south), results, tuple(fixed))

    zero = jnp.zeros((width, half), F32)
    results = jnp.zeros((count, width, order), F32)
    carry = (zero, zero, zero, zero, (zero, zero), results, (placed, *quarters))
    results = lax.fori_loop(0, trips, advance, carry)[5]
    first = results[:PIECES].reshape(columns, order)
    rest = results[PIECES:]
    partial_gram = lax.dot_general(
        first,
        first,
        (((1,), (1,)), ((), ())),
        precision=lax.Precision.HIGHEST,
        preferred_element_type=F32,
    )
    gram = summed(partial_gram, shape) / (nx * ny * order)
    lower = jnp.linalg.cholesky(gram)
    basis = jax.scipy.linalg.solve_triangular(lower, first, lower=True)
    traces = rest.reshape(batches - 1, columns, order)
    return (traces[None, None], basis[None, None], lower.T)


def solution(mesh):
    return jax.shard_map(
        functools.partial(body, (mesh.shape["gx"], mesh.shape["gy"])),
        mesh=mesh,
        in_specs=(
            P("gx", "gy", None, None),
            P("gx", "gy", None, None, None),
            P("gx", "gy", None),
            P(),
        ),
        out_specs=(P("gx", "gy", None, None, None), P("gx", "gy", None, None), P()),
        check_vma=False,
    )
```

```python
import functools

import jax
import jax.numpy as jnp
from jax import lax
from jax.experimental import pallas as pl
from jax.experimental.pallas import tpu as pltpu
from jax.sharding import PartitionSpec as P

PIECES = 2
UNROLL = 9
LIMIT = 8
VMEM = pl.BlockSpec(memory_space=pltpu.VMEM)
SMEM = pl.BlockSpec(memory_space=pltpu.SMEM)
HBM = pl.BlockSpec(memory_space=pltpu.HBM)
ANY = pl.BlockSpec(memory_space=pl.ANY)
F32 = jnp.float32
BF16 = jnp.bfloat16


def halves(value):
    high = value.astype(BF16)
    low = (value - high.astype(F32)).astype(BF16)
    return high, low


def product(value, high_ref, low_ref):
    rows = value.shape[0]
    high, low = halves(value)
    both = jnp.concatenate([high, low], axis=0)
    main = jnp.dot(both, high_ref[...], preferred_element_type=F32)
    rest = jnp.dot(high, low_ref[...], preferred_element_type=F32)
    return main[:rows] + (main[rows:] + rest)


def unwritten(*shapes):
    return pl.pallas_call(
        pass_through_kernel,
        out_shape=tuple(jax.ShapeDtypeStruct(shape, F32) for shape in shapes),
        out_specs=(ANY,) * len(shapes),
        compiler_params=params(4),
        name="unwritten",
    )()


def pass_through_kernel(*refs):
    del refs


def pass_through(*arrays):
    return pl.pallas_call(
        pass_through_kernel,
        out_shape=tuple(jax.ShapeDtypeStruct(a.shape, a.dtype) for a in arrays),
        in_specs=[ANY] * len(arrays),
        out_specs=(ANY,) * len(arrays),
        input_output_aliases={i: i for i in range(len(arrays))},
        compiler_params=params(4),
        name="pass_through",
    )(*arrays)


def params(mib):
    return pltpu.CompilerParams(vmem_limit_bytes=mib << 20)


def split_kernel(chunk, w_hbm, *refs):
    quarters, (buf, sem) = refs[:8], refs[8:]
    half = w_hbm.shape[0] // 2
    count = 2 * half // chunk

    def fetch(i):
        return pltpu.make_async_copy(
            w_hbm.at[pl.ds(i * chunk, chunk)], buf.at[i % 2], sem.at[i % 2]
        )

    fetch(0).start()
    for i in range(count):
        if i + 1 < count:
            fetch(i + 1).start()
        fetch(i).wait()
        high, low = halves(buf[i % 2])
        side, at = divmod(i * chunk, half)
        for j in range(2):
            cols = slice(j * half, (j + 1) * half)
            quarters[4 * side + 2 * j][at : at + chunk, :] = high[:, cols]
            quarters[4 * side + 2 * j + 1][at : at + chunk, :] = low[:, cols]


def split_operator(w):
    order = w.shape[0]
    half = order // 2
    chunk = half // 3
    shape = jax.ShapeDtypeStruct((half, half), BF16)
    return pl.pallas_call(
        functools.partial(split_kernel, chunk),
        out_shape=(shape,) * 8,
        in_specs=[HBM],
        out_specs=(VMEM,) * 8,
        scratch_shapes=[
            pltpu.VMEM((2, chunk, order), F32),
            pltpu.SemaphoreType.DMA((2,)),
        ],
        compiler_params=params(16),
        name="split_operator",
    )(w)


def when_active(offset, count, age_ref):
    age = age_ref[0] + offset
    piece = lax.div(age, 2)
    return (age >= 0) & (age < 2 * count) & (age == 2 * piece), piece


def south_kernel(offset, count, age_ref, placed_ref, south_ref, eh_ref, el_ref, nh_ref, nl_ref, out_ref):
    active, piece = when_active(offset, count, age_ref)
    half = south_ref.shape[1]

    @pl.when(active)
    def _():
        south = south_ref[...]
        out_ref[:, :half] = placed_ref[piece, :, :half] + product(south, eh_ref, el_ref)
        out_ref[:, half:] = placed_ref[piece, :, half:] + product(south, nh_ref, nl_ref)


def east_kernel(offset, count, age_ref, partial_ref, west_ref, high_ref, low_ref, out_ref):
    active, _ = when_active(offset, count, age_ref)
    half = west_ref.shape[1]

    @pl.when(active)
    def _():
        out_ref[...] = partial_ref[:, :half] + product(west_ref[...], high_ref, low_ref)


def north_kernel(offset, count, age_ref, partial_ref, west_ref, high_ref, low_ref, east_ref, *refs):
    out_ref, results_ref = refs[-2:]
    active, piece = when_active(offset, count, age_ref)
    half = west_ref.shape[1]

    @pl.when(active)
    def _():
        value = partial_ref[:, half:] + product(west_ref[...], high_ref, low_ref)
        out_ref[...] = value
        results_ref[piece, :, :half] = east_ref[...]
        results_ref[piece, :, half:] = value


def estimate(width, half, quarters):
    return pl.CostEstimate(
        flops=6 * quarters * width * half * half,
        bytes_accessed=1 << 20,
        transcendentals=0,
    )


def south_part(offset, count, age, placed, south, weights):
    _, width, order = placed.shape
    return pl.pallas_call(
        functools.partial(south_kernel, offset, count),
        out_shape=jax.ShapeDtypeStruct((width, order), F32),
        in_specs=[SMEM] + [VMEM] * 6,
        out_specs=VMEM,
        compiler_params=params(LIMIT),
        cost_estimate=estimate(width, order // 2, 2),
        name="south",
    )(age, placed, south, *weights)


def east_part(offset, count, age, partial, west, weights):
    width, half = west.shape
    return pl.pallas_call(
        functools.partial(east_kernel, offset, count),
        out_shape=jax.ShapeDtypeStruct((width, half), F32),
        in_specs=[SMEM] + [VMEM] * 4,
        out_specs=VMEM,
        compiler_params=params(LIMIT),
        cost_estimate=estimate(width, half, 1),
        name="east",
    )(age, partial, west, *weights)


def north_part(offset, count, age, partial, west, weights, east, results):
    width, half = west.shape
    return pl.pallas_call(
        functools.partial(north_kernel, offset, count),
        out_shape=(
            jax.ShapeDtypeStruct((width, half), F32),
            jax.ShapeDtypeStruct(results.shape, F32),
        ),
        in_specs=[SMEM] + [VMEM] * 6,
        out_specs=(VMEM, VMEM),
        input_output_aliases={6: 1},
        compiler_params=params(LIMIT),
        cost_estimate=estimate(width, half, 1),
        name="north",
    )(age, partial, west, *weights, east, results)


def summed(value, shape):
    for axis, size in (("gy", shape[1]), ("gx", shape[0])):
        apart = 1
        while apart < size:
            pairs = [(i, i ^ apart) for i in range(size)]
            value = value + lax.ppermute(value, axis, pairs)
            apart *= 2
    return value


def place_kernel(plan_ref, rows_ref, sources_ref, out_ref):
    batches, columns, placed_count = sources_ref.shape
    order = out_ref.shape[-1]
    at = lax.broadcasted_iota(jnp.int32, (order, placed_count), 0)
    placing = jnp.where(at == rows_ref[...], 1.0, 0.0).astype(BF16)
    for b in range(batches):
        source = sources_ref[plan_ref[b]]
        high, middle = halves(source)
        low = (source - high.astype(F32) - middle.astype(F32)).astype(BF16)
        parts = jnp.concatenate([high, middle, low], axis=0)
        spread = lax.dot_general(
            parts, placing, (((1,), (1,)), ((), ())), preferred_element_type=F32
        )
        out_ref[b] = spread[:columns] + (
            spread[columns : 2 * columns] + spread[2 * columns :]
        )


def place(plan, rows, sources, order):
    batches, columns, _ = sources.shape
    return pl.pallas_call(
        place_kernel,
        out_shape=jax.ShapeDtypeStruct((batches, columns, order), F32),
        in_specs=[SMEM, VMEM, VMEM],
        out_specs=VMEM,
        compiler_params=params(8),
        name="place",
    )(plan, rows, sources)


def sweep_pairs(shape, parity, dx, dy):
    nx, ny = shape
    return [
        (x * ny + y, (x + dx) * ny + y + dy)
        for x in range(nx - dx)
        for y in range(ny - dy)
        if (x + y) % 2 == parity
    ]


def body(shape, operators, sources, source_rows, batch_plan):
    nx, ny = shape
    axes = ("gx", "gy")
    depth = lax.axis_index("gx") + 3 * lax.axis_index("gy")
    order = operators.shape[-1]
    half = order // 2
    _, _, batches, columns, placed_count = sources.shape
    width = columns // PIECES
    count = batches * PIECES
    placed = place(batch_plan, source_rows[0], sources[0, 0], order)
    placed = placed.reshape(count, width, order)
    quarters = split_operator(operators[0, 0])

    steps = (nx - 1 + 3 * (ny - 1) + 2 * (count - 1)) // 2 + 1
    trips = -(-steps // UNROLL)

    def advance(trip, carry):
        west, south, results, fixed = carry
        fixed = pass_through(*fixed)
        placed, quarters = fixed[0], fixed[1:]
        age = (trip * (2 * UNROLL) - depth)[None].astype(jnp.int32)
        south = list(south)
        for offset in range(2 * UNROLL):
            parity = offset % 2
            partial = south_part(offset, count, age, placed, south[0], quarters[4:])
            to_east = east_part(offset, count, age, partial, west, quarters[:2])
            arrived = lax.ppermute(to_east, axes, sweep_pairs(shape, parity, 1, 0))
            to_north, results = north_part(
                offset, count, age, partial, west, quarters[2:4], to_east, results
            )
            risen = lax.ppermute(to_north, axes, sweep_pairs(shape, parity, 0, 1))
            west, south = arrived, south[1:] + [risen]
        return (west, tuple(south), results, tuple(fixed))

    zero = jnp.zeros((width, half), F32)
    (results,) = unwritten((count, width, order))
    carry = (zero, (zero, zero, zero), results, (placed, *quarters))
    results = lax.fori_loop(0, trips, advance, carry)[2]
    first = results[:PIECES].reshape(columns, order)
    rest = results[PIECES:]
    partial_gram = lax.dot_general(
        first,
        first,
        (((1,), (1,)), ((), ())),
        precision=lax.Precision.HIGHEST,
        preferred_element_type=F32,
    )
    gram = summed(partial_gram, shape) / (nx * ny * order)
    lower = jnp.linalg.cholesky(gram)
    basis = jax.scipy.linalg.solve_triangular(lower, first, lower=True)
    traces = rest.reshape(batches - 1, columns, order)
    return (traces[None, None], basis[None, None], lower.T)


def solution(mesh):
    return jax.shard_map(
        functools.partial(body, (mesh.shape["gx"], mesh.shape["gy"])),
        mesh=mesh,
        in_specs=(
            P("gx", "gy", None, None),
            P("gx", "gy", None, None, None),
            P("gx", "gy", None),
            P(),
        ),
        out_specs=(P("gx", "gy", None, None, None), P("gx", "gy", None, None), P()),
        check_vma=False,
    )
```

```python
import functools

import jax
import jax.numpy as jnp
from jax import lax
from jax.experimental import pallas as pl
from jax.experimental.pallas import tpu as pltpu
from jax.sharding import PartitionSpec as P

PIECES = 2
UNROLL = 8
LIMIT = 8
VMEM = pl.BlockSpec(memory_space=pltpu.VMEM)
SMEM = pl.BlockSpec(memory_space=pltpu.SMEM)
HBM = pl.BlockSpec(memory_space=pltpu.HBM)
ANY = pl.BlockSpec(memory_space=pl.ANY)
F32 = jnp.float32
BF16 = jnp.bfloat16


def halves(value):
    high = value.astype(BF16)
    low = (value - high.astype(F32)).astype(BF16)
    return high, low


def product(value, high_ref, low_ref):
    rows = value.shape[0]
    high, low = halves(value)
    both = jnp.concatenate([high, low], axis=0)
    main = jnp.dot(both, high_ref[...], preferred_element_type=F32)
    rest = jnp.dot(high, low_ref[...], preferred_element_type=F32)
    return main[:rows] + (main[rows:] + rest)


def unwritten(*shapes):
    return pl.pallas_call(
        pass_through_kernel,
        out_shape=tuple(jax.ShapeDtypeStruct(shape, F32) for shape in shapes),
        out_specs=(ANY,) * len(shapes),
        compiler_params=params(4),
        name="unwritten",
    )()


def pass_through_kernel(*refs):
    del refs


def pass_through(*arrays):
    return pl.pallas_call(
        pass_through_kernel,
        out_shape=tuple(jax.ShapeDtypeStruct(a.shape, a.dtype) for a in arrays),
        in_specs=[ANY] * len(arrays),
        out_specs=(ANY,) * len(arrays),
        input_output_aliases={i: i for i in range(len(arrays))},
        compiler_params=params(4),
        name="pass_through",
    )(*arrays)


def params(mib):
    return pltpu.CompilerParams(vmem_limit_bytes=mib << 20)


def split_kernel(chunk, w_hbm, *refs):
    quarters, (buf, sem) = refs[:8], refs[8:]
    half = w_hbm.shape[0] // 2
    count = 2 * half // chunk

    def fetch(i):
        return pltpu.make_async_copy(
            w_hbm.at[pl.ds(i * chunk, chunk)], buf.at[i % 2], sem.at[i % 2]
        )

    fetch(0).start()
    for i in range(count):
        if i + 1 < count:
            fetch(i + 1).start()
        fetch(i).wait()
        high, low = halves(buf[i % 2])
        side, at = divmod(i * chunk, half)
        for j in range(2):
            cols = slice(j * half, (j + 1) * half)
            quarters[4 * side + 2 * j][at : at + chunk, :] = high[:, cols]
            quarters[4 * side + 2 * j + 1][at : at + chunk, :] = low[:, cols]


def split_operator(w):
    order = w.shape[0]
    half = order // 2
    chunk = half // 3
    shape = jax.ShapeDtypeStruct((half, half), BF16)
    return pl.pallas_call(
        functools.partial(split_kernel, chunk),
        out_shape=(shape,) * 8,
        in_specs=[HBM],
        out_specs=(VMEM,) * 8,
        scratch_shapes=[
            pltpu.VMEM((2, chunk, order), F32),
            pltpu.SemaphoreType.DMA((2,)),
        ],
        compiler_params=params(16),
        name="split_operator",
    )(w)


def when_active(offset, count, age_ref):
    age = age_ref[0] + offset
    piece = lax.div(age, 2)
    return (age >= 0) & (age < 2 * count) & (age == 2 * piece), piece


def south_kernel(offset, count, age_ref, placed_ref, south_ref, eh_ref, el_ref, nh_ref, nl_ref, out_ref):
    active, piece = when_active(offset, count, age_ref)
    half = south_ref.shape[1]

    @pl.when(active)
    def _():
        south = south_ref[...]
        out_ref[:, :half] = placed_ref[piece, :, :half] + product(south, eh_ref, el_ref)
        out_ref[:, half:] = placed_ref[piece, :, half:] + product(south, nh_ref, nl_ref)


def east_kernel(offset, count, age_ref, partial_ref, west_ref, high_ref, low_ref, out_ref):
    active, _ = when_active(offset, count, age_ref)
    half = west_ref.shape[1]

    @pl.when(active)
    def _():
        out_ref[...] = partial_ref[:, :half] + product(west_ref[...], high_ref, low_ref)


def north_kernel(offset, count, age_ref, partial_ref, west_ref, high_ref, low_ref, east_ref, kept_ref, out_ref, results_ref):
    del kept_ref
    active, piece = when_active(offset, count, age_ref)
    half = west_ref.shape[1]

    @pl.when(active)
    def _():
        value = partial_ref[:, half:] + product(west_ref[...], high_ref, low_ref)
        out_ref[...] = value
        results_ref[piece, :, :half] = east_ref[...]
        results_ref[piece, :, half:] = value


def estimate(width, half, quarters):
    return pl.CostEstimate(
        flops=6 * quarters * width * half * half,
        bytes_accessed=1 << 20,
        transcendentals=0,
    )


def south_part(offset, count, age, placed, south, weights):
    _, width, order = placed.shape
    return pl.pallas_call(
        functools.partial(south_kernel, offset, count),
        out_shape=jax.ShapeDtypeStruct((width, order), F32),
        in_specs=[SMEM] + [VMEM] * 6,
        out_specs=VMEM,
        compiler_params=params(LIMIT),
        cost_estimate=estimate(width, order // 2, 2),
        name="south",
    )(age, placed, south, *weights)


def east_part(offset, count, age, partial, west, weights):
    width, half = west.shape
    return pl.pallas_call(
        functools.partial(east_kernel, offset, count),
        out_shape=jax.ShapeDtypeStruct((width, half), F32),
        in_specs=[SMEM] + [VMEM] * 4,
        out_specs=VMEM,
        compiler_params=params(LIMIT),
        cost_estimate=estimate(width, half, 1),
        name="east",
    )(age, partial, west, *weights)


def north_part(offset, count, age, partial, west, weights, east, results):
    width, half = west.shape
    return pl.pallas_call(
        functools.partial(north_kernel, offset, count),
        out_shape=(
            jax.ShapeDtypeStruct((width, half), F32),
            jax.ShapeDtypeStruct(results.shape, F32),
        ),
        in_specs=[SMEM] + [VMEM] * 6,
        out_specs=(VMEM, VMEM),
        input_output_aliases={6: 1},
        compiler_params=params(LIMIT),
        cost_estimate=estimate(width, half, 1),
        name="north",
    )(age, partial, west, *weights, east, results)


def summed(value, shape):
    for axis, size in (("gy", shape[1]), ("gx", shape[0])):
        apart = 1
        while apart < size:
            pairs = [(i, i ^ apart) for i in range(size)]
            value = value + lax.ppermute(value, axis, pairs)
            apart *= 2
    return value


def place_kernel(plan_ref, rows_ref, sources_ref, out_ref):
    batches, columns, placed_count = sources_ref.shape
    order = out_ref.shape[-1]
    at = lax.broadcasted_iota(jnp.int32, (order, placed_count), 0)
    placing = jnp.where(at == rows_ref[...], 1.0, 0.0).astype(BF16)
    for b in range(batches):
        source = sources_ref[plan_ref[b]]
        high, middle = halves(source)
        low = (source - high.astype(F32) - middle.astype(F32)).astype(BF16)
        parts = jnp.concatenate([high, middle, low], axis=0)
        spread = lax.dot_general(
            parts, placing, (((1,), (1,)), ((), ())), preferred_element_type=F32
        )
        out_ref[b] = spread[:columns] + (
            spread[columns : 2 * columns] + spread[2 * columns :]
        )


def place(plan, rows, sources, order):
    batches, columns, _ = sources.shape
    return pl.pallas_call(
        place_kernel,
        out_shape=jax.ShapeDtypeStruct((batches, columns, order), F32),
        in_specs=[SMEM, VMEM, VMEM],
        out_specs=VMEM,
        compiler_params=params(8),
        name="place",
    )(plan, rows, sources)


def sweep_pairs(shape, parity, dx, dy):
    nx, ny = shape
    return [
        (x * ny + y, (x + dx) * ny + y + dy)
        for x in range(parity, nx - dx, 2)
        for y in range(ny - dy)
    ]


def body(shape, operators, sources, source_rows, batch_plan):
    nx, ny = shape
    axes = ("gx", "gy")
    depth = lax.axis_index("gx") + 2 * lax.axis_index("gy")
    order = operators.shape[-1]
    half = order // 2
    _, _, batches, columns, placed_count = sources.shape
    width = columns // PIECES
    count = batches * PIECES
    placed = place(batch_plan, source_rows[0], sources[0, 0], order)
    placed = placed.reshape(count, width, order)
    quarters = split_operator(operators[0, 0])

    halves_needed = nx - 1 + 2 * (ny - 1) + 2 * (count - 1) + 1
    trips = -(-halves_needed // (2 * UNROLL))

    def advance(trip, carry):
        west, south, results, fixed = carry
        fixed = pass_through(*fixed)
        placed, quarters = fixed[0], fixed[1:]
        west, south = list(west), list(south)
        age = trip * (2 * UNROLL) - depth
        age_ref = age[None].astype(jnp.int32)
        for offset in range(2 * UNROLL):
            parity = offset % 2
            partial = south_part(
                offset, count, age_ref, placed, south[parity], quarters[4:]
            )
            to_east = east_part(
                offset, count, age_ref, partial, west[parity], quarters[:2]
            )
            arrived = lax.ppermute(to_east, axes, sweep_pairs(shape, parity, 1, 0))
            to_north, results = north_part(
                offset, count, age_ref, partial, west[parity], quarters[2:4], to_east, results
            )
            west[1 - parity] = arrived
            south[parity] = lax.ppermute(
                to_north, axes, sweep_pairs(shape, parity, 0, 1)
            )
        return (tuple(west), tuple(south), results, tuple(fixed))

    zero = jnp.zeros((width, half), F32)
    results, odd_west = unwritten((count, width, order), zero.shape)
    carry = ((zero, odd_west), (zero, zero), results, (placed, *quarters))
    ready = -(-(nx - 1 + 2 * (ny - 1) + 2 * (PIECES - 1) + 1) // (2 * UNROLL))
    carry = lax.fori_loop(0, ready, advance, carry)
    first = carry[2][:PIECES].reshape(columns, order)
    partial_gram = lax.dot_general(
        first,
        first,
        (((1,), (1,)), ((), ())),
        precision=lax.Precision.HIGHEST,
        preferred_element_type=F32,
    )
    gram = summed(partial_gram, shape) / (nx * ny * order)
    for trip in range(ready, trips):
        carry = advance(trip, carry)
    gram, first, results = lax.optimization_barrier((gram, first, carry[2]))
    rest = results[PIECES:]
    lower = jnp.linalg.cholesky(gram)
    basis = jax.scipy.linalg.solve_triangular(lower, first, lower=True)
    traces = rest.reshape(batches - 1, columns, order)
    return (traces[None, None], basis[None, None], lower.T)


def solution(mesh):
    return jax.shard_map(
        functools.partial(body, (mesh.shape["gx"], mesh.shape["gy"])),
        mesh=mesh,
        in_specs=(
            P("gx", "gy", None, None),
            P("gx", "gy", None, None, None),
            P("gx", "gy", None),
            P(),
        ),
        out_specs=(P("gx", "gy", None, None, None), P("gx", "gy", None, None), P()),
        check_vma=False,
    )
```

```python
import functools

import jax
import jax.numpy as jnp
from jax import lax
from jax.experimental import pallas as pl
from jax.experimental.pallas import tpu as pltpu
from jax.sharding import PartitionSpec as P

PIECES = 2
UNROLL = 8
LIMIT = 8
VMEM = pl.BlockSpec(memory_space=pltpu.VMEM)
SMEM = pl.BlockSpec(memory_space=pltpu.SMEM)
HBM = pl.BlockSpec(memory_space=pltpu.HBM)
ANY = pl.BlockSpec(memory_space=pl.ANY)
F32 = jnp.float32
BF16 = jnp.bfloat16


def halves(value):
    high = value.astype(BF16)
    low = (value - high.astype(F32)).astype(BF16)
    return high, low


def product(value, high_ref, low_ref):
    rows = value.shape[0]
    high, low = halves(value)
    both = jnp.concatenate([high, low], axis=0)
    main = jnp.dot(both, high_ref[...], preferred_element_type=F32)
    rest = jnp.dot(high, low_ref[...], preferred_element_type=F32)
    return main[:rows] + (main[rows:] + rest)


def unwritten(*shapes):
    return pl.pallas_call(
        nothing_kernel,
        out_shape=tuple(jax.ShapeDtypeStruct(shape, F32) for shape in shapes),
        out_specs=(ANY,) * len(shapes),
        compiler_params=params(4),
        name="unwritten",
    )()


def nothing_kernel(*refs):
    del refs


def params(mib):
    return pltpu.CompilerParams(vmem_limit_bytes=mib << 20)


def split_kernel(chunk, w_hbm, *refs):
    high_ref, low_ref, buf, sem = refs[-4:]
    count = w_hbm.shape[0] // chunk

    def fetch(i):
        return pltpu.make_async_copy(
            w_hbm.at[pl.ds(i * chunk, chunk)], buf.at[i % 2], sem.at[i % 2]
        )

    fetch(0).start()
    for i in range(count):
        if i + 1 < count:
            fetch(i + 1).start()
        fetch(i).wait()
        high, low = halves(buf[i % 2])
        high_ref[i * chunk : (i + 1) * chunk, :] = high
        low_ref[i * chunk : (i + 1) * chunk, :] = low


def split_operator(w, after):
    order = w.shape[0]
    chunk = order // 6
    shape = jax.ShapeDtypeStruct((order, order), BF16)
    return pl.pallas_call(
        functools.partial(split_kernel, chunk),
        out_shape=(shape, shape),
        in_specs=[HBM] + [ANY] * len(after),
        out_specs=(VMEM, VMEM),
        scratch_shapes=[
            pltpu.VMEM((2, chunk, order), F32),
            pltpu.SemaphoreType.DMA((2,)),
        ],
        compiler_params=params(16),
        name="split_operator",
    )(pltpu.with_memory_space_constraint(w, pltpu.HBM), *after)


def when_active(offset, count, age_ref):
    age = age_ref[0] + offset
    piece = lax.div(age, 2)
    return (age >= 0) & (age < 2 * count) & (age == 2 * piece), piece


def south_kernel(offset, count, age_ref, placed_ref, south_ref, high_ref, low_ref, out_ref):
    active, piece = when_active(offset, count, age_ref)
    half = south_ref.shape[1]

    @pl.when(active)
    def _():
        south = south_ref[...]
        out_ref[:, :half] = placed_ref[piece, :, :half] + product(
            south, high_ref.at[half:, :half], low_ref.at[half:, :half]
        )
        out_ref[:, half:] = placed_ref[piece, :, half:] + product(
            south, high_ref.at[half:, half:], low_ref.at[half:, half:]
        )


def east_kernel(offset, count, age_ref, partial_ref, west_ref, high_ref, low_ref, out_ref):
    active, _ = when_active(offset, count, age_ref)
    half = west_ref.shape[1]

    @pl.when(active)
    def _():
        out_ref[...] = partial_ref[:, :half] + product(
            west_ref[...], high_ref.at[:half, :half], low_ref.at[:half, :half]
        )


def north_kernel(offset, count, age_ref, partial_ref, west_ref, high_ref, low_ref, east_ref, kept_ref, out_ref, results_ref):
    del kept_ref
    active, piece = when_active(offset, count, age_ref)
    half = west_ref.shape[1]

    @pl.when(active)
    def _():
        value = partial_ref[:, half:] + product(
            west_ref[...], high_ref.at[:half, half:], low_ref.at[:half, half:]
        )
        out_ref[...] = value
        results_ref[piece, :, :half] = east_ref[...]
        results_ref[piece, :, half:] = value


def estimate(width, half, quarters):
    return pl.CostEstimate(
        flops=6 * quarters * width * half * half,
        bytes_accessed=1 << 20,
        transcendentals=0,
    )


def south_part(offset, count, age, placed, south, weights):
    _, width, order = placed.shape
    return pl.pallas_call(
        functools.partial(south_kernel, offset, count),
        out_shape=jax.ShapeDtypeStruct((width, order), F32),
        in_specs=[SMEM] + [VMEM] * 4,
        out_specs=VMEM,
        compiler_params=params(LIMIT),
        cost_estimate=estimate(width, order // 2, 2),
        name="south",
    )(age, placed, south, *weights)


def east_part(offset, count, age, partial, west, weights):
    width, half = west.shape
    return pl.pallas_call(
        functools.partial(east_kernel, offset, count),
        out_shape=jax.ShapeDtypeStruct((width, half), F32),
        in_specs=[SMEM] + [VMEM] * 4,
        out_specs=VMEM,
        compiler_params=params(LIMIT),
        cost_estimate=estimate(width, half, 1),
        name="east",
    )(age, partial, west, *weights)


def north_part(offset, count, age, partial, west, weights, east, results):
    width, half = west.shape
    return pl.pallas_call(
        functools.partial(north_kernel, offset, count),
        out_shape=(
            jax.ShapeDtypeStruct((width, half), F32),
            jax.ShapeDtypeStruct(results.shape, F32),
        ),
        in_specs=[SMEM] + [VMEM] * 6,
        out_specs=(VMEM, VMEM),
        input_output_aliases={6: 1},
        compiler_params=params(LIMIT),
        cost_estimate=estimate(width, half, 1),
        name="north",
    )(age, partial, west, *weights, east, results)


def summed(value, shape):
    for axis, size in (("gy", shape[1]), ("gx", shape[0])):
        apart = 1
        while apart < size:
            pairs = [(i, i ^ apart) for i in range(size)]
            value = value + lax.ppermute(value, axis, pairs)
            apart *= 2
    return value


def place_kernel(plan_ref, rows_ref, sources_ref, out_ref):
    batches, columns, placed_count = sources_ref.shape
    order = out_ref.shape[-1]
    at = lax.broadcasted_iota(jnp.int32, (order, placed_count), 0)
    placing = jnp.where(at == rows_ref[...], 1.0, 0.0).astype(BF16)
    for b in range(batches):
        source = sources_ref[plan_ref[b]]
        high, middle = halves(source)
        low = (source - high.astype(F32) - middle.astype(F32)).astype(BF16)
        parts = jnp.concatenate([high, middle, low], axis=0)
        spread = lax.dot_general(
            parts, placing, (((1,), (1,)), ((), ())), preferred_element_type=F32
        )
        out_ref[b] = spread[:columns] + (
            spread[columns : 2 * columns] + spread[2 * columns :]
        )


def place(plan, rows, sources, order):
    batches, columns, _ = sources.shape
    return pl.pallas_call(
        place_kernel,
        out_shape=jax.ShapeDtypeStruct((batches, columns, order), F32),
        in_specs=[SMEM, VMEM, VMEM],
        out_specs=VMEM,
        compiler_params=params(8),
        name="place",
    )(plan, rows, sources)


def sweep_pairs(shape, parity, dx, dy):
    nx, ny = shape
    return [
        (x * ny + y, (x + dx) * ny + y + dy)
        for x in range(parity, nx - dx, 2)
        for y in range(ny - dy)
    ]


def body(shape, operators, sources, source_rows, batch_plan):
    nx, ny = shape
    axes = ("gx", "gy")
    depth = lax.axis_index("gx") + 2 * lax.axis_index("gy")
    age = (-depth)[None].astype(jnp.int32)
    order = operators.shape[-1]
    half = order // 2
    _, _, batches, columns, placed_count = sources.shape
    width = columns // PIECES
    count = batches * PIECES
    placed = place(batch_plan, source_rows[0], sources[0, 0], order)
    placed = placed.reshape(count, width, order)
    zero = jnp.zeros((width, half), F32)
    weights = split_operator(operators[0, 0], (placed, zero))

    halves_needed = nx - 1 + 2 * (ny - 1) + 2 * (count - 1) + 1
    trips = -(-halves_needed // (2 * UNROLL))

    def advance(trip, carry):
        west, south, results, fixed = carry
        placed, weights = fixed[0], fixed[1:]
        west, south = list(west), list(south)


        for offset in range(2 * UNROLL * trip, 2 * UNROLL * (trip + 1)):
            parity = offset % 2
            partial = south_part(
                offset, count, age, placed, south[parity], weights
            )
            to_east = east_part(
                offset, count, age, partial, west[parity], weights
            )
            arrived = lax.ppermute(to_east, axes, sweep_pairs(shape, parity, 1, 0))
            to_north, results = north_part(
                offset, count, age, partial, west[parity], weights, to_east, results
            )
            west[1 - parity] = arrived
            south[parity] = lax.ppermute(
                to_north, axes, sweep_pairs(shape, parity, 0, 1)
            )
        return (tuple(west), tuple(south), results, tuple(fixed))

    results, odd_west = unwritten((count, width, order), zero.shape)
    carry = ((zero, odd_west), (zero, zero), results, (placed, *weights))
    ready = -(-(nx - 1 + 2 * (ny - 1) + 2 * (PIECES - 1) + 1) // (2 * UNROLL))
    for trip in range(ready):
        carry = advance(trip, carry)
    first = carry[2][:PIECES].reshape(columns, order)
    partial_gram = lax.dot_general(
        first,
        first,
        (((1,), (1,)), ((), ())),
        precision=lax.Precision.HIGHEST,
        preferred_element_type=F32,
    )
    gram = summed(partial_gram, shape) / (nx * ny * order)
    for trip in range(ready, trips):
        carry = advance(trip, carry)
    gram, first, results = lax.optimization_barrier((gram, first, carry[2]))
    rest = results[PIECES:]
    lower = jnp.linalg.cholesky(gram)
    basis = jax.scipy.linalg.solve_triangular(lower, first, lower=True)
    traces = rest.reshape(batches - 1, columns, order)
    return (traces[None, None], basis[None, None], lower.T)


def solution(mesh):
    return jax.shard_map(
        functools.partial(body, (mesh.shape["gx"], mesh.shape["gy"])),
        mesh=mesh,
        in_specs=(
            P("gx", "gy", None, None),
            P("gx", "gy", None, None, None),
            P("gx", "gy", None),
            P(),
        ),
        out_specs=(P("gx", "gy", None, None, None), P("gx", "gy", None, None), P()),
        check_vma=False,
    )
```

```python
import functools

import jax
import jax.numpy as jnp
from jax import lax
from jax.experimental import pallas as pl
from jax.experimental.pallas import tpu as pltpu
from jax.sharding import PartitionSpec as P

PIECES = 1
UNROLL = 9
LIMIT = 8
VMEM = pl.BlockSpec(memory_space=pltpu.VMEM)
SMEM = pl.BlockSpec(memory_space=pltpu.SMEM)
HBM = pl.BlockSpec(memory_space=pltpu.HBM)
ANY = pl.BlockSpec(memory_space=pl.ANY)
F32 = jnp.float32
BF16 = jnp.bfloat16


def halves(value):
    high = value.astype(BF16)
    low = (value - high.astype(F32)).astype(BF16)
    return high, low


def product(value, high_ref, low_ref):
    rows = value.shape[0]
    high, low = halves(value)
    both = jnp.concatenate([high, low], axis=0)
    main = jnp.dot(both, high_ref[...], preferred_element_type=F32)
    rest = jnp.dot(high, low_ref[...], preferred_element_type=F32)
    return main[:rows] + (main[rows:] + rest)


def unwritten(*shapes):
    return pl.pallas_call(
        nothing_kernel,
        out_shape=tuple(jax.ShapeDtypeStruct(shape, F32) for shape in shapes),
        out_specs=(ANY,) * len(shapes),
        compiler_params=params(4),
        name="unwritten",
    )()


def nothing_kernel(*refs):
    del refs


def params(mib):
    return pltpu.CompilerParams(vmem_limit_bytes=mib << 20)


def split_kernel(chunk, w_hbm, *refs):
    high_ref, low_ref, buf, sem = refs[-4:]
    count = w_hbm.shape[0] // chunk

    def fetch(i):
        return pltpu.make_async_copy(
            w_hbm.at[pl.ds(i * chunk, chunk)], buf.at[i % 2], sem.at[i % 2]
        )

    fetch(0).start()
    for i in range(count):
        if i + 1 < count:
            fetch(i + 1).start()
        fetch(i).wait()
        high, low = halves(buf[i % 2])
        high_ref[i * chunk : (i + 1) * chunk, :] = high
        low_ref[i * chunk : (i + 1) * chunk, :] = low


def split_operator(w, after):
    order = w.shape[0]
    chunk = order // 6
    shape = jax.ShapeDtypeStruct((order, order), BF16)
    return pl.pallas_call(
        functools.partial(split_kernel, chunk),
        out_shape=(shape, shape),
        in_specs=[HBM] + [ANY] * len(after),
        out_specs=(VMEM, VMEM),
        scratch_shapes=[
            pltpu.VMEM((2, chunk, order), F32),
            pltpu.SemaphoreType.DMA((2,)),
        ],
        compiler_params=params(16),
        name="split_operator",
    )(pltpu.with_memory_space_constraint(w, pltpu.HBM), *after)


def when_active(offset, count, age_ref):
    age = age_ref[0] + offset
    piece = lax.div(age, 2)
    return (age >= 0) & (age < 2 * count) & (age == 2 * piece), piece


def south_kernel(offset, count, age_ref, placed_ref, south_ref, high_ref, low_ref, out_ref):
    active, piece = when_active(offset, count, age_ref)
    half = south_ref.shape[1]

    @pl.when(active)
    def _():
        south = south_ref[...]
        out_ref[:, :half] = placed_ref[piece, :, :half] + product(
            south, high_ref.at[half:, :half], low_ref.at[half:, :half]
        )
        out_ref[:, half:] = placed_ref[piece, :, half:] + product(
            south, high_ref.at[half:, half:], low_ref.at[half:, half:]
        )


def east_kernel(offset, count, age_ref, partial_ref, west_ref, high_ref, low_ref, out_ref):
    active, _ = when_active(offset, count, age_ref)
    half = west_ref.shape[1]

    @pl.when(active)
    def _():
        out_ref[...] = partial_ref[:, :half] + product(
            west_ref[...], high_ref.at[:half, :half], low_ref.at[:half, :half]
        )


def north_kernel(offset, count, age_ref, partial_ref, west_ref, high_ref, low_ref, east_ref, kept_ref, out_ref, results_ref):
    del kept_ref
    active, piece = when_active(offset, count, age_ref)
    half = west_ref.shape[1]

    @pl.when(active)
    def _():
        value = partial_ref[:, half:] + product(
            west_ref[...], high_ref.at[:half, half:], low_ref.at[:half, half:]
        )
        out_ref[...] = value
        results_ref[piece, :, :half] = east_ref[...]
        results_ref[piece, :, half:] = value


def estimate(width, half, quarters):
    return pl.CostEstimate(
        flops=6 * quarters * width * half * half,
        bytes_accessed=1 << 20,
        transcendentals=0,
    )


def south_part(offset, count, age, placed, south, weights):
    _, width, order = placed.shape
    return pl.pallas_call(
        functools.partial(south_kernel, offset, count),
        out_shape=jax.ShapeDtypeStruct((width, order), F32),
        in_specs=[SMEM] + [VMEM] * 4,
        out_specs=VMEM,
        compiler_params=params(LIMIT),
        cost_estimate=estimate(width, order // 2, 2),
        name="south",
    )(age, placed, south, *weights)


def east_part(offset, count, age, partial, west, weights):
    width, half = west.shape
    return pl.pallas_call(
        functools.partial(east_kernel, offset, count),
        out_shape=jax.ShapeDtypeStruct((width, half), F32),
        in_specs=[SMEM] + [VMEM] * 4,
        out_specs=VMEM,
        compiler_params=params(LIMIT),
        cost_estimate=estimate(width, half, 1),
        name="east",
    )(age, partial, west, *weights)


def north_part(offset, count, age, partial, west, weights, east, results):
    width, half = west.shape
    return pl.pallas_call(
        functools.partial(north_kernel, offset, count),
        out_shape=(
            jax.ShapeDtypeStruct((width, half), F32),
            jax.ShapeDtypeStruct(results.shape, F32),
        ),
        in_specs=[SMEM] + [VMEM] * 6,
        out_specs=(VMEM, VMEM),
        input_output_aliases={6: 1},
        compiler_params=params(LIMIT),
        cost_estimate=estimate(width, half, 1),
        name="north",
    )(age, partial, west, *weights, east, results)


def summed(value, shape):
    for axis, size in (("gy", shape[1]), ("gx", shape[0])):
        apart = 1
        while apart < size:
            pairs = [(i, i ^ apart) for i in range(size)]
            value = value + lax.ppermute(value, axis, pairs)
            apart *= 2
    return value


def place_kernel(plan_ref, rows_ref, sources_ref, out_ref):
    batches, columns, placed_count = sources_ref.shape
    order = out_ref.shape[-1]
    at = lax.broadcasted_iota(jnp.int32, (order, placed_count), 0)
    placing = jnp.where(at == rows_ref[...], 1.0, 0.0).astype(BF16)
    for b in range(batches):
        source = sources_ref[plan_ref[b]]
        high, middle = halves(source)
        low = (source - high.astype(F32) - middle.astype(F32)).astype(BF16)
        parts = jnp.concatenate([high, middle, low], axis=0)
        spread = lax.dot_general(
            parts, placing, (((1,), (1,)), ((), ())), preferred_element_type=F32
        )
        out_ref[b] = spread[:columns] + (
            spread[columns : 2 * columns] + spread[2 * columns :]
        )


def place(plan, rows, sources, order):
    batches, columns, _ = sources.shape
    return pl.pallas_call(
        place_kernel,
        out_shape=jax.ShapeDtypeStruct((batches, columns, order), F32),
        in_specs=[SMEM, VMEM, VMEM],
        out_specs=VMEM,
        compiler_params=params(8),
        name="place",
    )(plan, rows, sources)


def sweep_pairs(shape, parity, dx, dy):
    nx, ny = shape
    return [
        (x * ny + y, (x + dx) * ny + y + dy)
        for x in range(parity, nx - dx, 2)
        for y in range(ny - dy)
    ]


def body(shape, operators, sources, source_rows, batch_plan):
    nx, ny = shape
    axes = ("gx", "gy")
    depth = lax.axis_index("gx") + 2 * lax.axis_index("gy")
    age = (-depth)[None].astype(jnp.int32)
    order = operators.shape[-1]
    half = order // 2
    _, _, batches, columns, placed_count = sources.shape
    width = columns // PIECES
    count = batches * PIECES
    placed = place(batch_plan, source_rows[0], sources[0, 0], order)
    placed = placed.reshape(count, width, order)
    zero = jnp.zeros((width, half), F32)
    weights = split_operator(operators[0, 0], (placed, zero))

    halves_needed = nx - 1 + 2 * (ny - 1) + 2 * (count - 1) + 1
    trips = -(-halves_needed // (2 * UNROLL))

    def advance(trip, carry):
        west, south, results, fixed = carry
        placed, weights = fixed[0], fixed[1:]
        west, south = list(west), list(south)


        for offset in range(2 * UNROLL * trip, 2 * UNROLL * (trip + 1)):
            parity = offset % 2
            partial = south_part(
                offset, count, age, placed, south[parity], weights
            )
            to_east = east_part(
                offset, count, age, partial, west[parity], weights
            )
            arrived = lax.ppermute(to_east, axes, sweep_pairs(shape, parity, 1, 0))
            to_north, results = north_part(
                offset, count, age, partial, west[parity], weights, to_east, results
            )
            west[1 - parity] = arrived
            south[parity] = lax.ppermute(
                to_north, axes, sweep_pairs(shape, parity, 0, 1)
            )
        return (tuple(west), tuple(south), results, tuple(fixed))

    results, odd_west = unwritten((count, width, order), zero.shape)
    carry = ((zero, odd_west), (zero, zero), results, (placed, *weights))
    ready = -(-(nx - 1 + 2 * (ny - 1) + 2 * (PIECES - 1) + 1) // (2 * UNROLL))
    for trip in range(ready):
        carry = advance(trip, carry)
    first = carry[2][:PIECES].reshape(columns, order)
    partial_gram = lax.dot_general(
        first,
        first,
        (((1,), (1,)), ((), ())),
        precision=lax.Precision.HIGHEST,
        preferred_element_type=F32,
    )
    gram = summed(partial_gram, shape) / (nx * ny * order)
    for trip in range(ready, trips):
        carry = advance(trip, carry)
    gram, first, results = lax.optimization_barrier((gram, first, carry[2]))
    rest = results[PIECES:]
    lower = jnp.linalg.cholesky(gram)
    basis = jax.scipy.linalg.solve_triangular(lower, first, lower=True)
    traces = rest.reshape(batches - 1, columns, order)
    return (traces[None, None], basis[None, None], lower.T)


def solution(mesh):
    return jax.shard_map(
        functools.partial(body, (mesh.shape["gx"], mesh.shape["gy"])),
        mesh=mesh,
        in_specs=(
            P("gx", "gy", None, None),
            P("gx", "gy", None, None, None),
            P("gx", "gy", None),
            P(),
        ),
        out_specs=(P("gx", "gy", None, None, None), P("gx", "gy", None, None), P()),
        check_vma=False,
    )
```
